32 devices in a mesh: dp: 8 (over z, core), mp: 4 (over y, x).
Axes of the slice: x: 2, y: 2, z: 4, core: 2. Of those that a mesh axis runs over, the one named last changes fastest.
Arguments:
- tokens: bfloat16 [2048, 3072], P('dp'), may hold values from -60 to 60
- ln_gain: float32 [3072], replicated, may hold values from 0.25 to 1.75
- q_weight: bfloat16 [3072, 4096], P('dp', 'mp'), may hold values from -1 to 1
- k_weight: bfloat16 [3072, 4096], P('dp', 'mp'), may hold values from -1 to 1
- v_weight: bfloat16 [3072, 4096], P('dp', 'mp'), may hold values from -0.109375 to 0.109375
- q_gain: float32 [4096], P('mp'), may hold values from 0.6 to 6
- k_gain: float32 [4096], P('mp'), may hold values from 0.6 to 6
- out_weight: bfloat16 [3072, 4096], P('dp', 'mp'), may hold values from -0.25 to 0.25
Outputs:
- mixed: bfloat16 [2048, 3072], P(('dp', 'mp'))
The draws below stay inside these ranges and needn't reach their ends.
All inputs are finite; a program needn't handle non-finite values.
Results may differ from the reference program's by a relative error of at most 0.018.
Values may be sent and summed in bfloat16 or wider, within the bound.
A program may use at most 128 MiB of HBM per device.

```python
import math
import jax
import jax.numpy as jnp
from jax import lax

D = 3072
HEADS = 32
HEAD_DIM = 128
IMG_TOKENS = 256
TOKENS = 2048
N_MP = 4


def draw_tokens(key, part):
    base = jax.random.normal(jax.random.fold_in(key, 21), (TOKENS, D), jnp.float32)
    result = base
    return jnp.clip(result, -60.0, 60.0).astype(jnp.bfloat16)


def weight_pair(key):
    shape = (D, HEADS * HEAD_DIM)
    first = jnp.clip(jax.random.normal(jax.random.fold_in(key, 31), shape, jnp.float32), -4.0, 4.0) * D ** (-0.5)
    second = jnp.clip(jax.random.normal(jax.random.fold_in(key, 32), shape, jnp.float32), -4.0, 4.0) * D ** (-0.5)
    return (first, second)


def draw_q_weight(key, part):
    return weight_pair(key)[0].astype(jnp.bfloat16)


def draw_k_weight(key, part):
    return weight_pair(key)[1].astype(jnp.bfloat16)


def gain_draw(key):
    return jax.random.uniform(key, (HEADS * HEAD_DIM,), jnp.float32, 0.6, 1.4)


def draw_q_gain(key, part):
    return gain_draw(jax.random.fold_in(key, 41))


def draw_k_gain(key, part):
    return gain_draw(jax.random.fold_in(key, 42))


def steps_of(own_key, shape, shards, smallest, largest):
    loudness = 1.0
    for axis_at, parts in shards:
        heights = jax.random.uniform(jax.random.fold_in(jax.random.fold_in(own_key, 6), axis_at), (parts,), jnp.float32, smallest / len(shards), largest / len(shards))
        loudness = loudness * jnp.repeat(jnp.exp(heights), shape[axis_at] // parts).reshape((-1,) + (1,) * (len(shape) - 1 - axis_at))
    return loudness


def gaussian(own_key, dims, width, reach, cuts=(), kind=jnp.bfloat16):
    entries = jax.random.normal(own_key, dims, jnp.float32) * width
    if len(cuts) > 0:
        entries = steps_of(own_key, dims, cuts, -0.22, 0.18) * entries
    return jnp.clip(entries, min=-reach, max=reach).astype(kind)


def setup_inputs(seed: int = 0) -> dict:
    splits = jax.random.split(jax.random.key(seed), 9)
    return {
        "tokens": draw_tokens(jax.random.fold_in(splits[8], 71), 0),
        "ln_gain": jnp.clip(1.0 + 0.15 * jax.random.normal(splits[1], (D,), jnp.float32), 0.25, 1.75),
        "q_weight": draw_q_weight(jax.random.fold_in(splits[8], 71), 0),
        "k_weight": draw_k_weight(jax.random.fold_in(splits[8], 71), 0),
        "v_weight": gaussian(splits[4], (D, HEADS * HEAD_DIM), D ** -0.5, 0.109375, ((0, 8), (1, 4))),
        "q_gain": draw_q_gain(jax.random.fold_in(splits[8], 71), 0),
        "k_gain": draw_k_gain(jax.random.fold_in(splits[8], 71), 0),
        "out_weight": gaussian(splits[7], (D, HEADS * HEAD_DIM), (HEADS * HEAD_DIM // 8) ** -0.5, 0.25, ((0, 8), (1, 4))),
    }


epsilon = 1e-06

def layer_norm(values, scale_gain):
    average = lax.optimization_barrier(jnp.mean(values, axis=-1, keepdims=True))
    centred = values - average
    variance = lax.optimization_barrier(jnp.mean(centred * centred, axis=-1, keepdims=True))
    return centred * lax.rsqrt(variance + epsilon) * scale_gain

def head_norm(projected, scale_gain):
    heads_count = projected.shape[1] // HEAD_DIM
    shaped = projected.reshape(projected.shape[0], heads_count, HEAD_DIM)
    normed = layer_norm(shaped, scale_gain.reshape(heads_count, HEAD_DIM))
    return normed.reshape(projected.shape).astype(jnp.bfloat16)

def attend_image(triple):
    queries = triple[0].astype(jnp.float32)
    key_rows = triple[1].astype(jnp.float32)
    value_rows = triple[2].astype(jnp.float32)
    scores = jnp.einsum('qhd,khd->hqk', queries, key_rows) * (1.0 / math.sqrt(HEAD_DIM))
    highest = lax.optimization_barrier(jnp.max(scores, axis=-1, keepdims=True))
    weights = jnp.exp(scores - highest)
    probs = (weights / lax.optimization_barrier(jnp.sum(weights, axis=-1, keepdims=True))).astype(jnp.bfloat16)
    context = jnp.einsum('hqk,khd->qhd', probs.astype(jnp.float32), value_rows)
    return context.astype(jnp.bfloat16)

def reference(tokens, ln_gain, q_weight, k_weight, v_weight, q_gain, k_gain, out_weight):
    normed = layer_norm(tokens.astype(jnp.float32), ln_gain).astype(jnp.bfloat16)
    queries = jnp.dot(normed, q_weight, preferred_element_type=jnp.float32)
    key_rows = jnp.dot(normed, k_weight, preferred_element_type=jnp.float32)
    value_rows = jnp.dot(normed, v_weight, preferred_element_type=jnp.float32).astype(jnp.bfloat16)
    query_normed = head_norm(queries, q_gain)
    key_normed = head_norm(key_rows, k_gain)
    images = TOKENS // IMG_TOKENS
    shaped = (images, IMG_TOKENS, HEADS, HEAD_DIM)
    context = lax.map(attend_image, (query_normed.reshape(shaped), key_normed.reshape(shaped), value_rows.reshape(shaped)))
    context = context.reshape(TOKENS, HEADS * HEAD_DIM)
    group_width = HEADS * HEAD_DIM // N_MP
    context_groups = context.reshape(TOKENS, N_MP, group_width).transpose(1, 0, 2)
    weight_groups = out_weight.reshape(D, N_MP, group_width).transpose(1, 0, 2)

    def add_group(total, paired):
        partial_sum = lax.dot_general(paired[0], paired[1], (((1,), (1,)), ((), ())), preferred_element_type=jnp.float32)
        rounded = lax.optimization_barrier(partial_sum.astype(jnp.bfloat16))
        return (total + rounded.astype(jnp.float32), None)
    total, unused = lax.scan(add_group, jnp.zeros((TOKENS, D), jnp.float32), (context_groups, weight_groups))
    return total.astype(jnp.bfloat16)
```

```python
import functools
import math

import jax
import jax.numpy as jnp
from jax import lax
from jax.experimental import pallas as pl
from jax.experimental.pallas import tpu as pltpu
from jax.sharding import PartitionSpec as P

HEAD_DIM = 128
IMG_TOKENS = 256


epsilon = 1e-06


def layer_norm(values, scale_gain):
    average = jnp.mean(values, axis=-1, keepdims=True)
    centred = values - average
    variance = jnp.mean(centred * centred, axis=-1, keepdims=True)
    return centred * lax.rsqrt(variance + epsilon) * scale_gain


def head_norm(projected, scale_gain):
    heads_count = projected.shape[1] // HEAD_DIM
    shaped = projected.reshape(projected.shape[0], heads_count, HEAD_DIM)
    normed = layer_norm(shaped, scale_gain.reshape(heads_count, HEAD_DIM))
    return normed.reshape(projected.shape).astype(jnp.bfloat16)


def attend(queries, key_rows, value_rows):
    scores = jnp.einsum(
        "bqhd,bkhd->bhqk", queries, key_rows, preferred_element_type=jnp.float32
    ) * (1.0 / math.sqrt(HEAD_DIM))
    highest = jnp.max(scores, axis=-1, keepdims=True)
    weights = jnp.exp(scores - highest)
    probs = (weights / jnp.sum(weights, axis=-1, keepdims=True)).astype(jnp.bfloat16)
    context = jnp.einsum("bhqk,bkhd->bqhd", probs, value_rows, preferred_element_type=jnp.float32)
    return context.astype(jnp.bfloat16)


def place_three(holder, pieces, offset, local_width):
    holder = lax.dynamic_update_slice(holder, pieces[0], (offset, 0))
    holder = lax.dynamic_update_slice(holder, pieces[1], (offset, local_width))
    return lax.dynamic_update_slice(holder, pieces[2], (offset, 2 * local_width))


def gathered_weights(tokens, ln_gain, q_weight, k_weight, v_weight, q_gain, k_gain, out_weight):
    normed = layer_norm(tokens.astype(jnp.float32), ln_gain).astype(jnp.bfloat16)
    token_count = normed.shape[0]
    local_width = q_weight.shape[1]
    feature_count = normed.shape[1]
    stacked = jnp.zeros((feature_count, 3 * local_width), jnp.bfloat16)
    projections = place_three(
        stacked,
        (
            lax.all_gather(q_weight, "dp", axis=0, tiled=True),
            lax.all_gather(k_weight, "dp", axis=0, tiled=True),
            lax.all_gather(v_weight, "dp", axis=0, tiled=True),
        ),
        jnp.int32(0),
        local_width,
    )
    combined = jnp.dot(normed, projections, preferred_element_type=jnp.float32)
    queries = combined[:, :local_width]
    key_rows = combined[:, local_width : 2 * local_width]
    value_cast = combined[:, 2 * local_width :].astype(jnp.bfloat16)
    query_normed = head_norm(queries, q_gain)
    key_normed = head_norm(key_rows, k_gain)
    images = token_count // IMG_TOKENS
    shaped = (images, IMG_TOKENS, local_width // HEAD_DIM, HEAD_DIM)
    context = attend(
        query_normed.reshape(shaped), key_normed.reshape(shaped), value_cast.reshape(shaped)
    )
    context = context.reshape(token_count, local_width)
    out_full = lax.all_gather(out_weight, "dp", axis=0, tiled=True)
    return lax.psum_scatter(
        lax.dot_general(
            context, out_full, (((1,), (1,)), ((), ())), preferred_element_type=jnp.float32
        ).astype(jnp.bfloat16),
        "mp",
        scatter_dimension=0,
        tiled=True,
    )


MESH = pl.DeviceIdType.MESH


def exchange_kernel(
    pairs, groups, tokens, ln_gain, q_w, k_w, v_w, q_gain, k_gain, out_w, result,
    raw, normed, weights, out_rows, projected, context, partial, arrived, summed, final,
    local_sem, up_send, down_send, token_recv, peer_send, peer_recv,
    w_send, w_recv, own_send, own_recv, pass_send, pass_recv, out_send, out_recv,
    c_up, c_down, c_recv, p_send, p_recv, f_send, f_recv,
):
    dp = lax.axis_index("dp")
    group = lax.axis_index("mp")
    pair = dp // 2
    core = dp % 2
    rows = tokens.shape[0]
    part = rows // groups
    shard = q_w.shape[0]
    width = q_w.shape[1] // pairs
    span = 2 * shard

    def at_pair(other):
        return (other * 2 + core, group)

    partner = (pair * 2 + (1 - core), group)

    def at_group(other):
        return (dp, other)

    def remote(source, target, send, recv, device):
        return pltpu.make_async_remote_copy(
            src_ref=source, dst_ref=target, send_sem=send, recv_sem=recv,
            device_id=device, device_id_type=MESH,
        )

    greeted = pltpu.get_barrier_semaphore()
    for step in range(1, pairs):
        pl.semaphore_signal(
            greeted, inc=1, device_id=at_pair((pair + step) % pairs), device_id_type=MESH
        )
    for step in range(1, groups):
        pl.semaphore_signal(
            greeted, inc=1, device_id=at_group((group + step) % groups), device_id_type=MESH
        )
    pl.semaphore_signal(greeted, inc=1, device_id=partner, device_id_type=MESH)

    projections = (q_w, k_w, v_w)
    own_columns = pl.ds(pl.multiple_of(pair * width, width), width)
    quarter = pl.ds(pl.multiple_of(group * part, part), part)
    locals_ = [pltpu.make_async_copy(tokens, raw.at[pair], local_sem.at[0])]
    for t in range(3):
        locals_.append(
            pltpu.make_async_copy(
                projections[t].at[:, own_columns],
                weights.at[pair, core, :, pl.ds(t * width, width)],
                local_sem.at[1 + t],
            )
        )
    locals_.append(pltpu.make_async_copy(out_w, out_rows.at[core], local_sem.at[4]))
    for copy in locals_:
        copy.start()
    pl.semaphore_wait(greeted, pairs + groups - 1)

    def first_hop(up):
        return remote(
            tokens.at[quarter, :], raw.at[pair, quarter, :],
            (up_send if up else down_send).at[pair], token_recv.at[pair],
            at_pair(pair + 1 if up else pair - 1),
        )

    def next_hop(block, up):
        return remote(
            raw.at[block, quarter, :], raw.at[block, quarter, :],
            (up_send if up else down_send).at[block], token_recv.at[block],
            at_pair(pair + 1 if up else pair - 1),
        )

    def to_peer(block, step):
        return remote(
            raw.at[block, quarter, :], raw.at[block, quarter, :],
            peer_send.at[block, step - 1], peer_recv.at[block, group],
            at_group((group + step) % groups),
        )

    def from_peer(block, step):
        other = (group + step) % groups
        there = raw.at[block, pl.ds(pl.multiple_of(other * part, part), part), :]
        return remote(
            there, there, peer_send.at[block, step - 1], peer_recv.at[block, other],
            at_group(other),
        )

    def weight_to(other, t):
        return remote(
            projections[t].at[:, pl.ds(pl.multiple_of(other * width, width), width)],
            weights.at[pair, core, :, pl.ds(t * width, width)],
            w_send.at[other, t], w_recv.at[pair, t], at_pair(other),
        )

    def weight_from(other, t):
        there = weights.at[other, core, :, pl.ds(t * width, width)]
        return remote(there, there, w_send.at[other, t], w_recv.at[other, t], at_pair(other))

    def own_weight(t):
        return remote(
            projections[t].at[:, own_columns],
            weights.at[pair, core, :, pl.ds(t * width, width)],
            own_send.at[t], own_recv.at[t], partner,
        )

    def partner_weight(t):
        there = weights.at[pair, 1 - core, :, pl.ds(t * width, width)]
        return remote(there, there, own_send.at[t], own_recv.at[t], partner)

    def pass_on(other):
        return remote(
            weights.at[other, core], weights.at[other, core],
            pass_send.at[other], pass_recv.at[other], partner,
        )

    def passed(other):
        there = weights.at[other, 1 - core]
        return remote(there, there, pass_send.at[other], pass_recv.at[other], partner)

    def out_over():
        return remote(out_w, out_rows.at[core], out_send, out_recv, partner)

    def out_back():
        there = out_rows.at[1 - core]
        return remote(there, there, out_send, out_recv, partner)

    has_up = pair + 1 < pairs
    has_down = pair > 0

    @pl.when(has_up)
    def _():
        first_hop(True).start()

    @pl.when(has_down)
    def _():
        first_hop(False).start()

    def send_weights(t):
        for distance in range(pairs - 1, 0, -1):
            @pl.when(pair + distance < pairs)
            def _():
                weight_to(pair + distance, t).start()

            @pl.when(pair - distance >= 0)
            def _():
                weight_to(pair - distance, t).start()

    send_weights(0)
    for t in range(3):
        own_weight(t).start()
    out_over().start()

    def normalise(block):
        @pl.loop(0, rows // 16)
        def _(chunk):
            place = pl.ds(pl.multiple_of(chunk * 16, 16), 16)
            values = raw[block, place, :].astype(jnp.float32)
            average = jnp.mean(values, axis=-1, keepdims=True)
            centred = values - average
            variance = jnp.mean(centred * centred, axis=-1, keepdims=True)
            scaled = centred * lax.rsqrt(variance + epsilon) * ln_gain[...]
            scaled = scaled.astype(jnp.bfloat16)
            for p in range(pairs):
                normed[p, block, place, :] = scaled[:, p * span : (p + 1) * span]

    for copy in locals_:
        copy.wait()
    normalise(pair)

    def relay(block, up):
        next_hop(block, up).wait_recv()

        @pl.when(has_up if up else has_down)
        def _():
            next_hop(block, up).start()

        for step in range(1, groups):
            to_peer(block, step).start()

    for distance in range(1, pairs):
        @pl.when(pair - distance >= 0)
        def _():
            relay(pair - distance, True)

        @pl.when(pair + distance < pairs)
        def _():
            relay(pair + distance, False)

        if distance < 3:
            send_weights(distance)
    for t in range(pairs, 3):
        send_weights(t)

    def project(block, first):
        @pl.loop(0, pairs)
        def _(image):
            product = jnp.dot(
                normed[block, image], weights[block].reshape(span, 3 * width),
                preferred_element_type=jnp.float32,
            )
            projected[image] = product if first else projected[image] + product

    @pl.loop(1, pairs)
    def _(k):
        block = (pair + k) % pairs
        for step in range(1, groups):
            from_peer(block, step).wait_recv()
        normalise(block)

    for t in range(3):
        partner_weight(t).wait_recv()
    project(pair, True)

    @pl.loop(1, pairs)
    def _(k):
        block = (pair + k) % pairs
        for t in range(3):
            weight_from(block, t).wait_recv()
        pass_on(block).start()

    @pl.loop(1, pairs)
    def _(k):
        block = (pair + k) % pairs
        passed(block).wait_recv()
        project(block, False)

    def head_layer_norm(values, scale_gain):
        average = jnp.mean(values, axis=-1, keepdims=True)
        centred = values - average
        variance = jnp.mean(centred * centred, axis=-1, keepdims=True)
        return (centred * lax.rsqrt(variance + epsilon) * scale_gain).astype(jnp.bfloat16)

    def context_hop(block, image, up):
        return remote(
            context.at[block, image], context.at[block, image],
            (c_up if up else c_down).at[block, image], c_recv.at[block, image],
            at_pair(pair + 1 if up else pair - 1),
        )

    @pl.loop(0, pairs)
    def _(image):
        for h in range(width // HEAD_DIM):
            lanes = slice(h * HEAD_DIM, (h + 1) * HEAD_DIM)
            queries = head_layer_norm(projected[image, :, lanes], q_gain[pair, :, lanes])
            shifted = slice(width + h * HEAD_DIM, width + (h + 1) * HEAD_DIM)
            key_rows = head_layer_norm(projected[image, :, shifted], k_gain[pair, :, lanes])
            last = slice(2 * width + h * HEAD_DIM, 2 * width + (h + 1) * HEAD_DIM)
            value_rows = projected[image, :, last].astype(jnp.bfloat16)
            scores = lax.dot_general(
                queries, key_rows, (((1,), (1,)), ((), ())), preferred_element_type=jnp.float32
            ) * (1.0 / math.sqrt(HEAD_DIM))
            highest = jnp.max(scores, axis=-1, keepdims=True)
            spread = jnp.exp(scores - highest)
            probs = (spread / jnp.sum(spread, axis=-1, keepdims=True)).astype(jnp.bfloat16)
            mixed = jnp.dot(probs, value_rows, preferred_element_type=jnp.float32)
            context[pair, image, :, lanes] = mixed.astype(jnp.bfloat16)

        @pl.when(has_up)
        def _():
            context_hop(pair, image, True).start()

        @pl.when(has_down)
        def _():
            context_hop(pair, image, False).start()

    def pass_context(block, image, up):
        context_hop(block, image, up).wait_recv()

        @pl.when(has_up if up else has_down)
        def _():
            context_hop(block, image, up).start()

    def partial_to(image, step):
        other = (group + step) % groups
        return remote(
            partial.at[image, pl.ds(pl.multiple_of(other * part, part), part), :],
            arrived.at[image, group],
            p_send.at[image, step - 1], p_recv.at[image, group], at_group(other),
        )

    def partial_from(image, step):
        other = (group + step) % groups
        there = arrived.at[image, other]
        return remote(there, there, p_send.at[image, step - 1], p_recv.at[image, other], at_group(other))

    out_back().wait_recv()

    @pl.loop(0, pairs)
    def _(image):
        for distance in range(1, pairs):
            @pl.when(pair - distance >= 0)
            def _():
                pass_context(pair - distance, image, True)

            @pl.when(pair + distance < pairs)
            def _():
                pass_context(pair + distance, image, False)

        for c in range(2):
            total = None
            for p in range(pairs):
                product = lax.dot_general(
                    context[p, image], out_rows[c, :, p * width : (p + 1) * width],
                    (((1,), (1,)), ((), ())), preferred_element_type=jnp.float32,
                )
                total = product if total is None else total + product
            partial[image, :, c * shard : (c + 1) * shard] = total.astype(jnp.bfloat16)
        for step in range(1, groups):
            partial_to(image, step).start()

    def final_to(image):
        return remote(
            summed.at[image], final.at[pair], f_send.at[image], f_recv.at[pair], at_pair(image)
        )

    def final_from(other):
        return remote(
            final.at[other], final.at[other], f_send.at[other], f_recv.at[other], at_pair(other)
        )

    @pl.loop(0, pairs)
    def _(image):
        total = partial[image, quarter, :].astype(jnp.float32)
        for step in range(1, groups):
            partial_from(image, step).wait_recv()
            total = total + arrived[image, (group + step) % groups].astype(jnp.float32)
        summed[image] = total.astype(jnp.bfloat16)

        @pl.when(image != pair)
        def _():
            final_to(image).start()

        @pl.when(image == pair)
        def _():
            final[pair] = summed[image]

    @pl.loop(1, pairs)
    def _(k):
        final_from((pair + k) % pairs).wait_recv()

    for p in range(pairs):
        result[:, p * span : (p + 1) * span] = final[p]

    @pl.when(has_up)
    def _():
        first_hop(True).wait_send()

    @pl.when(has_down)
    def _():
        first_hop(False).wait_send()

    for t in range(3):
        own_weight(t).wait_send()
    out_over().wait_send()
    for distance in range(1, pairs):
        for up in (True, False):
            inside = pair - distance >= 0 if up else pair + distance < pairs
            block = pair - distance if up else pair + distance

            @pl.when(inside & (has_up if up else has_down))
            def _():
                next_hop(block, up).wait_send()

                @pl.loop(0, pairs)
                def _(image):
                    context_hop(block, image, up).wait_send()

    @pl.loop(0, pairs)
    def _(image):
        @pl.when(has_up)
        def _():
            context_hop(pair, image, True).wait_send()

        @pl.when(has_down)
        def _():
            context_hop(pair, image, False).wait_send()

        for step in range(1, groups):
            partial_to(image, step).wait_send()

    @pl.loop(1, pairs)
    def _(k):
        block = (pair + k) % pairs
        for t in range(3):
            weight_to(block, t).wait_send()
        pass_on(block).wait_send()
        for step in range(1, groups):
            to_peer(block, step).wait_send()
        final_to(block).wait_send()


def exchanged_heads(pairs, groups, tokens, ln_gain, q_w, k_w, v_w, q_gain, k_gain, out_w):
    rows, features = tokens.shape
    shard, local_width = q_w.shape
    width = local_width // pairs
    part = rows // groups
    dma = pltpu.SemaphoreType.DMA
    in_hbm = pl.BlockSpec(memory_space=pl.ANY)
    in_vmem = pl.BlockSpec(memory_space=pltpu.VMEM)
    bf16 = jnp.bfloat16
    return pl.pallas_call(
        functools.partial(exchange_kernel, pairs, groups),
        out_shape=jax.ShapeDtypeStruct((part, features), bf16),
        in_specs=[in_hbm, in_vmem, in_hbm, in_hbm, in_hbm, in_vmem, in_vmem, in_hbm],
        out_specs=in_vmem,
        scratch_shapes=[
            pltpu.VMEM((pairs, rows, features), bf16),
            pltpu.VMEM((pairs, pairs, rows, 2 * shard), bf16),
            pltpu.VMEM((pairs, 2, shard, 3 * width), bf16),
            pltpu.VMEM((2, shard, local_width), bf16),
            pltpu.VMEM((pairs, rows, 3 * width), jnp.float32),
            pltpu.VMEM((pairs, pairs, rows, width), bf16),
            pltpu.VMEM((pairs, rows, 2 * shard), bf16),
            pltpu.VMEM((pairs, groups, part, 2 * shard), bf16),
            pltpu.VMEM((pairs, part, 2 * shard), bf16),
            pltpu.VMEM((pairs, part, 2 * shard), bf16),
            dma((5,)), dma((pairs,)), dma((pairs,)), dma((pairs,)),
            dma((pairs, groups)), dma((pairs, groups)),
            dma((pairs, 3)), dma((pairs, 3)), dma((3,)), dma((3,)),
            dma((pairs,)), dma((pairs,)), dma, dma,
            dma((pairs, pairs)), dma((pairs, pairs)), dma((pairs, pairs)),
            dma((pairs, groups)), dma((pairs, groups)), dma((pairs,)), dma((pairs,)),
        ],
        compiler_params=pltpu.CompilerParams(
            collective_id=0, has_side_effects=True, vmem_limit_bytes=60 * 1024 * 1024
        ),
    )(
        tokens, ln_gain.reshape(1, features), q_w, k_w, v_w,
        q_gain.reshape(pairs, 1, width), k_gain.reshape(pairs, 1, width), out_w,
    )


def on_device(tokens, ln_gain, q_w, k_w, v_w, q_gain, k_gain, out_w):
    devices = lax.axis_size("dp")
    groups = lax.axis_size("mp")
    pairs = devices // 2
    fits = (
        devices % 2 == 0
        and pairs > 1
        and q_w.shape[1] % (pairs * HEAD_DIM) == 0
        and q_w.shape[0] % 128 == 0
        and tokens.shape[0] == IMG_TOKENS
        and tokens.shape[0] % (16 * groups) == 0
        and pairs <= 4
    )
    if fits:
        return exchanged_heads(pairs, groups, tokens, ln_gain, q_w, k_w, v_w, q_gain, k_gain, out_w)
    return gathered_weights(tokens, ln_gain, q_w, k_w, v_w, q_gain, k_gain, out_w)


def solution(mesh):
    in_specs = (
        P("dp", None),
        P(),
        P("dp", "mp"),
        P("dp", "mp"),
        P("dp", "mp"),
        P("mp"),
        P("mp"),
        P("dp", "mp"),
    )
    out_specs = P(("dp", "mp"), None)
    return jax.shard_map(
        on_device, mesh=mesh, in_specs=in_specs, out_specs=out_specs, check_vma=False
    )
```

```python
import functools
import math

import jax
import jax.numpy as jnp
from jax import lax
from jax.experimental import pallas as pl
from jax.experimental.pallas import tpu as pltpu
from jax.sharding import PartitionSpec as P

HEAD_DIM = 128
IMG_TOKENS = 256


epsilon = 1e-06


def layer_norm(values, scale_gain):
    average = jnp.mean(values, axis=-1, keepdims=True)
    centred = values - average
    variance = jnp.mean(centred * centred, axis=-1, keepdims=True)
    return centred * lax.rsqrt(variance + epsilon) * scale_gain


def head_norm(projected, scale_gain):
    heads_count = projected.shape[1] // HEAD_DIM
    shaped = projected.reshape(projected.shape[0], heads_count, HEAD_DIM)
    normed = layer_norm(shaped, scale_gain.reshape(heads_count, HEAD_DIM))
    return normed.reshape(projected.shape).astype(jnp.bfloat16)


def attend(queries, key_rows, value_rows):
    scores = jnp.einsum(
        "bqhd,bkhd->bhqk", queries, key_rows, preferred_element_type=jnp.float32
    ) * (1.0 / math.sqrt(HEAD_DIM))
    highest = jnp.max(scores, axis=-1, keepdims=True)
    weights = jnp.exp(scores - highest)
    probs = (weights / jnp.sum(weights, axis=-1, keepdims=True)).astype(jnp.bfloat16)
    context = jnp.einsum("bhqk,bkhd->bqhd", probs, value_rows, preferred_element_type=jnp.float32)
    return context.astype(jnp.bfloat16)


def place_three(holder, pieces, offset, local_width):
    holder = lax.dynamic_update_slice(holder, pieces[0], (offset, 0))
    holder = lax.dynamic_update_slice(holder, pieces[1], (offset, local_width))
    return lax.dynamic_update_slice(holder, pieces[2], (offset, 2 * local_width))


def gathered_weights(tokens, ln_gain, q_weight, k_weight, v_weight, q_gain, k_gain, out_weight):
    normed = layer_norm(tokens.astype(jnp.float32), ln_gain).astype(jnp.bfloat16)
    token_count = normed.shape[0]
    local_width = q_weight.shape[1]
    feature_count = normed.shape[1]
    stacked = jnp.zeros((feature_count, 3 * local_width), jnp.bfloat16)
    projections = place_three(
        stacked,
        (
            lax.all_gather(q_weight, "dp", axis=0, tiled=True),
            lax.all_gather(k_weight, "dp", axis=0, tiled=True),
            lax.all_gather(v_weight, "dp", axis=0, tiled=True),
        ),
        jnp.int32(0),
        local_width,
    )
    combined = jnp.dot(normed, projections, preferred_element_type=jnp.float32)
    queries = combined[:, :local_width]
    key_rows = combined[:, local_width : 2 * local_width]
    value_cast = combined[:, 2 * local_width :].astype(jnp.bfloat16)
    query_normed = head_norm(queries, q_gain)
    key_normed = head_norm(key_rows, k_gain)
    images = token_count // IMG_TOKENS
    shaped = (images, IMG_TOKENS, local_width // HEAD_DIM, HEAD_DIM)
    context = attend(
        query_normed.reshape(shaped), key_normed.reshape(shaped), value_cast.reshape(shaped)
    )
    context = context.reshape(token_count, local_width)
    out_full = lax.all_gather(out_weight, "dp", axis=0, tiled=True)
    return lax.psum_scatter(
        lax.dot_general(
            context, out_full, (((1,), (1,)), ((), ())), preferred_element_type=jnp.float32
        ).astype(jnp.bfloat16),
        "mp",
        scatter_dimension=0,
        tiled=True,
    )


MESH = pl.DeviceIdType.MESH


def exchange_kernel(
    pairs, groups, tokens, ln_gain, q_w, k_w, v_w, q_gain, k_gain, out_w, result,
    raw, normed, weights, out_rows, context, partial, arrived, summed, final,
    local_sem, up_send, down_send, token_recv, peer_send, peer_recv,
    w_send, w_recv, own_send, own_recv, pass_send, pass_recv, out_send, out_recv,
    c_up, c_down, c_recv, p_send, p_recv, f_send, f_recv,
):
    dp = lax.axis_index("dp")
    group = lax.axis_index("mp")
    pair = dp // 2
    core = dp % 2
    rows = tokens.shape[0]
    part = rows // groups
    shard = q_w.shape[0]
    width = q_w.shape[1] // pairs
    span = 2 * shard
    heads = width // HEAD_DIM

    def at_pair(other):
        return (other * 2 + core, group)

    partner = (pair * 2 + (1 - core), group)

    def at_group(other):
        return (dp, other)

    def remote(source, target, send, recv, device):
        return pltpu.make_async_remote_copy(
            src_ref=source, dst_ref=target, send_sem=send, recv_sem=recv,
            device_id=device, device_id_type=MESH,
        )

    greeted = pltpu.get_barrier_semaphore()
    for step in range(1, pairs):
        pl.semaphore_signal(
            greeted, inc=1, device_id=at_pair((pair + step) % pairs), device_id_type=MESH
        )
    for step in range(1, groups):
        pl.semaphore_signal(
            greeted, inc=1, device_id=at_group((group + step) % groups), device_id_type=MESH
        )
    pl.semaphore_signal(greeted, inc=1, device_id=partner, device_id_type=MESH)

    projections = (q_w, k_w, v_w)

    def columns(other, h, t):
        start = pl.multiple_of(other * width + h * HEAD_DIM, HEAD_DIM)
        return projections[t].at[:, pl.ds(start, HEAD_DIM)]

    def slot(h, block, side, t):
        return weights.at[h, block, side, :, pl.ds(t * HEAD_DIM, HEAD_DIM)]

    quarter = pl.ds(pl.multiple_of(group * part, part), part)
    locals_ = [pltpu.make_async_copy(tokens, raw.at[pair], local_sem.at[0])]
    locals_.append(pltpu.make_async_copy(out_w, out_rows.at[core], local_sem.at[1]))
    for h in range(heads):
        for t in range(3):
            locals_.append(
                pltpu.make_async_copy(
                    columns(pair, h, t), slot(h, pair, core, t), local_sem.at[2 + 3 * h + t]
                )
            )
    for copy in locals_:
        copy.start()
    pl.semaphore_wait(greeted, pairs + groups - 1)

    def first_hop(up):
        return remote(
            tokens.at[quarter, :], raw.at[pair, quarter, :],
            (up_send if up else down_send).at[pair], token_recv.at[pair],
            at_pair(pair + 1 if up else pair - 1),
        )

    def next_hop(block, up):
        return remote(
            raw.at[block, quarter, :], raw.at[block, quarter, :],
            (up_send if up else down_send).at[block], token_recv.at[block],
            at_pair(pair + 1 if up else pair - 1),
        )

    beside = group + 1 - 2 * (group % 2)
    across = (group + 2) % 4
    first = jnp.where(core == 0, beside, across)
    second = jnp.where(core == 0, across, beside)
    opposite = 3 - group

    def part_of(block, other):
        return raw.at[block, pl.ds(pl.multiple_of(other * part, part), part), :]

    def peer_copy(block, owner, place, other):
        there = part_of(block, owner)
        return remote(
            there, there, peer_send.at[block, place], peer_recv.at[block, owner], at_group(other)
        )

    def to_first(block):
        return peer_copy(block, group, 0, first)

    def to_second(block):
        return peer_copy(block, group, 1, second)

    def cross(block):
        return peer_copy(block, first, 2, second)

    def from_peer(block, owner):
        return peer_copy(block, owner, 0, first)

    def weight_to(other, h, t):
        return remote(
            columns(other, h, t), slot(h, pair, core, t),
            w_send.at[other, h, t], w_recv.at[pair, h, t], at_pair(other),
        )

    def weight_from(other, h, t):
        there = slot(h, other, core, t)
        return remote(there, there, w_send.at[other, h, t], w_recv.at[other, h, t], at_pair(other))

    def own_weight(h, t):
        return remote(
            columns(pair, h, t), slot(h, pair, core, t), own_send.at[h, t], own_recv.at[h, t], partner
        )

    def partner_weight(h, t):
        there = slot(h, pair, 1 - core, t)
        return remote(there, there, own_send.at[h, t], own_recv.at[h, t], partner)

    def pass_on(other, h):
        there = weights.at[h, other, core]
        return remote(there, there, pass_send.at[other, h], pass_recv.at[other, h], partner)

    def passed(other, h):
        there = weights.at[h, other, 1 - core]
        return remote(there, there, pass_send.at[other, h], pass_recv.at[other, h], partner)

    def out_over():
        return remote(out_w, out_rows.at[core], out_send, out_recv, partner)

    def out_back():
        there = out_rows.at[1 - core]
        return remote(there, there, out_send, out_recv, partner)

    has_up = pair + 1 < pairs
    has_down = pair > 0

    @pl.when(has_up)
    def _():
        first_hop(True).start()

    @pl.when(has_down)
    def _():
        first_hop(False).start()

    def send_weights(up, some):
        for h in some:
            for distance in range(pairs - 1, 0, -1) if h == 0 else range(1, pairs):
                other = pair + distance if up else pair - distance

                @pl.when(other < pairs if up else other >= 0)
                def _():
                    for t in range(3):
                        weight_to(other, h, t).start()

    @pl.when(pair == 0)
    def _():
        send_weights(True, range(1))

    @pl.when(pair == pairs - 1)
    def _():
        send_weights(False, range(1))

    for h in range(heads):
        for t in range(3):
            own_weight(h, t).start()
    out_over().start()

    def normalise(block):
        @pl.loop(0, rows // 16)
        def _(chunk):
            place = pl.ds(pl.multiple_of(chunk * 16, 16), 16)
            values = raw[block, place, :].astype(jnp.float32)
            average = jnp.mean(values, axis=-1, keepdims=True)
            centred = values - average
            variance = jnp.mean(centred * centred, axis=-1, keepdims=True)
            scaled = centred * lax.rsqrt(variance + epsilon) * ln_gain[...]
            scaled = scaled.astype(jnp.bfloat16)
            for p in range(pairs):
                normed[p, block, place, :] = scaled[:, p * span : (p + 1) * span]

    for copy in locals_:
        copy.wait()
    normalise(pair)

    def relay(block, up):
        next_hop(block, up).wait_recv()

        @pl.when(has_up if up else has_down)
        def _():
            next_hop(block, up).start()

        to_first(block).start()
        to_second(block).start()

    for distance in range(1, pairs):
        @pl.when(pair - distance >= 0)
        def _():
            relay(pair - distance, True)

        @pl.when(pair + distance < pairs)
        def _():
            relay(pair + distance, False)

        @pl.when(has_up & (pair == distance))
        def _():
            send_weights(True, range(1))

        @pl.when(has_down & (pair == pairs - 1 - distance))
        def _():
            send_weights(False, range(1))

    def cross_tokens(block):
        from_peer(block, first).wait_recv()
        cross(block).start()

    for distance in range(1, pairs):
        @pl.when(pair - distance >= 0)
        def _():
            cross_tokens(pair - distance)

        @pl.when(pair + distance < pairs)
        def _():
            cross_tokens(pair + distance)

    send_weights(True, range(1, heads))
    send_weights(False, range(1, heads))

    def take_tokens(block):
        from_peer(block, second).wait_recv()
        from_peer(block, opposite).wait_recv()
        normalise(block)

    def pass_weights(h):
        @pl.loop(1, pairs)
        def _(k):
            block = (pair + k) % pairs
            for t in range(3):
                weight_from(block, h, t).wait_recv()
            pass_on(block, h).start()

    for distance in range(1, pairs):
        if distance == pairs - 1:
            pass_weights(0)

        @pl.when(pair - distance >= 0)
        def _():
            take_tokens(pair - distance)

        @pl.when(pair + distance < pairs)
        def _():
            take_tokens(pair + distance)

    def head_layer_norm(values, scale_gain):
        average = jnp.mean(values, axis=-1, keepdims=True)
        centred = values - average
        variance = jnp.mean(centred * centred, axis=-1, keepdims=True)
        return (centred * lax.rsqrt(variance + epsilon) * scale_gain).astype(jnp.bfloat16)

    def context_hop(block, image, h, up):
        there = context.at[block, image, :, pl.ds(h * HEAD_DIM, HEAD_DIM)]
        return remote(
            there, there,
            (c_up if up else c_down).at[block, image, h], c_recv.at[block, image, h],
            at_pair(pair + 1 if up else pair - 1),
        )

    def pass_context(image, h, distance):
        for up in (True, False):
            block = pair - distance if up else pair + distance

            @pl.when(block >= 0 if up else block < pairs)
            def _():
                context_hop(block, image, h, up).wait_recv()

                @pl.when(has_up if up else has_down)
                def _():
                    context_hop(block, image, h, up).start()

    for h in range(heads):
        if h > 0:
            pass_weights(h)
        for t in range(3):
            partner_weight(h, t).wait_recv()

        @pl.loop(1, pairs)
        def _(k):
            passed((pair + k) % pairs, h).wait_recv()

        lanes = slice(h * HEAD_DIM, (h + 1) * HEAD_DIM)

        @pl.loop(0, pairs)
        def _(image):
            total = None
            for p in range(pairs):
                product = jnp.dot(
                    normed[p, image], weights[h, p].reshape(span, 3 * HEAD_DIM),
                    preferred_element_type=jnp.float32,
                )
                total = product if total is None else total + product
            queries = head_layer_norm(total[:, :HEAD_DIM], q_gain[pair, :, lanes])
            key_rows = head_layer_norm(total[:, HEAD_DIM : 2 * HEAD_DIM], k_gain[pair, :, lanes])
            value_rows = total[:, 2 * HEAD_DIM :].astype(jnp.bfloat16)
            scores = lax.dot_general(
                queries, key_rows, (((1,), (1,)), ((), ())), preferred_element_type=jnp.float32
            ) * (1.0 / math.sqrt(HEAD_DIM))
            highest = jnp.max(scores, axis=-1, keepdims=True)
            spread = jnp.exp(scores - highest)
            probs = (spread / jnp.sum(spread, axis=-1, keepdims=True)).astype(jnp.bfloat16)
            mixed = jnp.dot(probs, value_rows, preferred_element_type=jnp.float32)
            context[pair, image, :, lanes] = mixed.astype(jnp.bfloat16)

            @pl.when(has_up)
            def _():
                context_hop(pair, image, h, True).start()

            @pl.when(has_down)
            def _():
                context_hop(pair, image, h, False).start()

            if h > 0:
                pass_context(image, h - 1, 1)

    for distance in range(1, pairs):
        @pl.loop(0, pairs)
        def _(image):
            for h in range(heads):
                hop = distance + (1 if h < heads - 1 else 0)
                if hop < pairs and not (distance == pairs - 1 and h == heads - 1):
                    pass_context(image, h, hop)

    def partial_to(image, step):
        other = (group + step) % groups
        return remote(
            partial.at[image, pl.ds(pl.multiple_of(other * part, part), part), :],
            arrived.at[image, group],
            p_send.at[image, step - 1], p_recv.at[image, group], at_group(other),
        )

    def partial_from(image, step):
        other = (group + step) % groups
        there = arrived.at[image, other]
        return remote(there, there, p_send.at[image, step - 1], p_recv.at[image, other], at_group(other))

    out_back().wait_recv()

    @pl.loop(0, pairs)
    def _(image):
        pass_context(image, heads - 1, pairs - 1)

        for c in range(2):
            total = None
            for p in range(pairs):
                product = lax.dot_general(
                    context[p, image], out_rows[c, :, p * width : (p + 1) * width],
                    (((1,), (1,)), ((), ())), preferred_element_type=jnp.float32,
                )
                total = product if total is None else total + product
            partial[image, :, c * shard : (c + 1) * shard] = total.astype(jnp.bfloat16)
        for step in range(1, groups):
            partial_to(image, step).start()

    def final_to(image):
        return remote(
            summed.at[image], final.at[pair], f_send.at[image], f_recv.at[pair], at_pair(image)
        )

    def final_from(other):
        return remote(
            final.at[other], final.at[other], f_send.at[other], f_recv.at[other], at_pair(other)
        )

    @pl.loop(0, pairs)
    def _(image):
        total = partial[image, quarter, :].astype(jnp.float32)
        for step in range(1, groups):
            partial_from(image, step).wait_recv()
            total = total + arrived[image, (group + step) % groups].astype(jnp.float32)
        summed[image] = total.astype(jnp.bfloat16)

        @pl.when(image != pair)
        def _():
            final_to(image).start()

        @pl.when(image == pair)
        def _():
            final[pair] = summed[image]

    @pl.loop(1, pairs)
    def _(k):
        final_from((pair + k) % pairs).wait_recv()

    for p in range(pairs):
        result[:, p * span : (p + 1) * span] = final[p]

    @pl.when(has_up)
    def _():
        first_hop(True).wait_send()

    @pl.when(has_down)
    def _():
        first_hop(False).wait_send()

    for h in range(heads):
        for t in range(3):
            own_weight(h, t).wait_send()
    out_over().wait_send()
    for distance in range(1, pairs):
        for up in (True, False):
            inside = pair - distance >= 0 if up else pair + distance < pairs
            block = pair - distance if up else pair + distance

            @pl.when(inside & (has_up if up else has_down))
            def _():
                next_hop(block, up).wait_send()

                @pl.loop(0, pairs)
                def _(image):
                    for h in range(heads):
                        context_hop(block, image, h, up).wait_send()

    @pl.loop(0, pairs)
    def _(image):
        @pl.when(has_up)
        def _():
            for h in range(heads):
                context_hop(pair, image, h, True).wait_send()

        @pl.when(has_down)
        def _():
            for h in range(heads):
                context_hop(pair, image, h, False).wait_send()

        for step in range(1, groups):
            partial_to(image, step).wait_send()

    @pl.loop(1, pairs)
    def _(k):
        block = (pair + k) % pairs
        for h in range(heads):
            for t in range(3):
                weight_to(block, h, t).wait_send()
            pass_on(block, h).wait_send()
        to_first(block).wait_send()
        to_second(block).wait_send()
        cross(block).wait_send()
        final_to(block).wait_send()


def exchanged_heads(pairs, groups, tokens, ln_gain, q_w, k_w, v_w, q_gain, k_gain, out_w):
    rows, features = tokens.shape
    shard, local_width = q_w.shape
    width = local_width // pairs
    heads = width // HEAD_DIM
    part = rows // groups
    dma = pltpu.SemaphoreType.DMA
    in_hbm = pl.BlockSpec(memory_space=pl.ANY)
    in_vmem = pl.BlockSpec(memory_space=pltpu.VMEM)
    bf16 = jnp.bfloat16
    return pl.pallas_call(
        functools.partial(exchange_kernel, pairs, groups),
        out_shape=jax.ShapeDtypeStruct((part, features), bf16),
        in_specs=[in_hbm, in_vmem, in_hbm, in_hbm, in_hbm, in_vmem, in_vmem, in_hbm],
        out_specs=in_vmem,
        scratch_shapes=[
            pltpu.VMEM((pairs, rows, features), bf16),
            pltpu.VMEM((pairs, pairs, rows, 2 * shard), bf16),
            pltpu.VMEM((heads, pairs, 2, shard, 3 * HEAD_DIM), bf16),
            pltpu.VMEM((2, shard, local_width), bf16),
            pltpu.VMEM((pairs, pairs, rows, width), bf16),
            pltpu.VMEM((pairs, rows, 2 * shard), bf16),
            pltpu.VMEM((pairs, groups, part, 2 * shard), bf16),
            pltpu.VMEM((pairs, part, 2 * shard), bf16),
            pltpu.VMEM((pairs, part, 2 * shard), bf16),
            dma((2 + 3 * heads,)), dma((pairs,)), dma((pairs,)), dma((pairs,)),
            dma((pairs, groups)), dma((pairs, groups)),
            dma((pairs, heads, 3)), dma((pairs, heads, 3)), dma((heads, 3)), dma((heads, 3)),
            dma((pairs, heads)), dma((pairs, heads)), dma, dma,
            dma((pairs, pairs, heads)), dma((pairs, pairs, heads)), dma((pairs, pairs, heads)),
            dma((pairs, groups)), dma((pairs, groups)), dma((pairs,)), dma((pairs,)),
        ],
        compiler_params=pltpu.CompilerParams(
            collective_id=0, has_side_effects=True, vmem_limit_bytes=60 * 1024 * 1024
        ),
    )(
        tokens, ln_gain.reshape(1, features), q_w, k_w, v_w,
        q_gain.reshape(pairs, 1, width), k_gain.reshape(pairs, 1, width), out_w,
    )


def on_device(tokens, ln_gain, q_w, k_w, v_w, q_gain, k_gain, out_w):
    devices = lax.axis_size("dp")
    groups = lax.axis_size("mp")
    pairs = devices // 2
    fits = (
        devices % 2 == 0
        and pairs > 1
        and groups == 4
        and q_w.shape[1] % (pairs * HEAD_DIM) == 0
        and q_w.shape[0] % 128 == 0
        and tokens.shape[0] == IMG_TOKENS
        and tokens.shape[0] % (16 * groups) == 0
        and pairs <= 4
        and q_w.shape[1] <= 2 * pairs * HEAD_DIM
    )
    if fits:
        return exchanged_heads(pairs, groups, tokens, ln_gain, q_w, k_w, v_w, q_gain, k_gain, out_w)
    return gathered_weights(tokens, ln_gain, q_w, k_w, v_w, q_gain, k_gain, out_w)


def solution(mesh):
    in_specs = (
        P("dp", None),
        P(),
        P("dp", "mp"),
        P("dp", "mp"),
        P("dp", "mp"),
        P("mp"),
        P("mp"),
        P("dp", "mp"),
    )
    out_specs = P(("dp", "mp"), None)
    return jax.shard_map(
        on_device, mesh=mesh, in_specs=in_specs, out_specs=out_specs, check_vma=False
    )
```

```python
import functools
import math

import jax
import jax.numpy as jnp
from jax import lax
from jax.experimental import pallas as pl
from jax.experimental.pallas import tpu as pltpu
from jax.sharding import PartitionSpec as P

HEAD_DIM = 128
IMG_TOKENS = 256


epsilon = 1e-06


def layer_norm(values, scale_gain):
    average = jnp.mean(values, axis=-1, keepdims=True)
    centred = values - average
    variance = jnp.mean(centred * centred, axis=-1, keepdims=True)
    return centred * lax.rsqrt(variance + epsilon) * scale_gain


def head_norm(projected, scale_gain):
    heads_count = projected.shape[1] // HEAD_DIM
    shaped = projected.reshape(projected.shape[0], heads_count, HEAD_DIM)
    normed = layer_norm(shaped, scale_gain.reshape(heads_count, HEAD_DIM))
    return normed.reshape(projected.shape).astype(jnp.bfloat16)


def attend(queries, key_rows, value_rows):
    scores = jnp.einsum(
        "bqhd,bkhd->bhqk", queries, key_rows, preferred_element_type=jnp.float32
    ) * (1.0 / math.sqrt(HEAD_DIM))
    highest = jnp.max(scores, axis=-1, keepdims=True)
    weights = jnp.exp(scores - highest)
    probs = (weights / jnp.sum(weights, axis=-1, keepdims=True)).astype(jnp.bfloat16)
    context = jnp.einsum("bhqk,bkhd->bqhd", probs, value_rows, preferred_element_type=jnp.float32)
    return context.astype(jnp.bfloat16)


def place_three(holder, pieces, offset, local_width):
    holder = lax.dynamic_update_slice(holder, pieces[0], (offset, 0))
    holder = lax.dynamic_update_slice(holder, pieces[1], (offset, local_width))
    return lax.dynamic_update_slice(holder, pieces[2], (offset, 2 * local_width))


def gathered_weights(tokens, ln_gain, q_weight, k_weight, v_weight, q_gain, k_gain, out_weight):
    normed = layer_norm(tokens.astype(jnp.float32), ln_gain).astype(jnp.bfloat16)
    token_count = normed.shape[0]
    local_width = q_weight.shape[1]
    feature_count = normed.shape[1]
    stacked = jnp.zeros((feature_count, 3 * local_width), jnp.bfloat16)
    projections = place_three(
        stacked,
        (
            lax.all_gather(q_weight, "dp", axis=0, tiled=True),
            lax.all_gather(k_weight, "dp", axis=0, tiled=True),
            lax.all_gather(v_weight, "dp", axis=0, tiled=True),
        ),
        jnp.int32(0),
        local_width,
    )
    combined = jnp.dot(normed, projections, preferred_element_type=jnp.float32)
    queries = combined[:, :local_width]
    key_rows = combined[:, local_width : 2 * local_width]
    value_cast = combined[:, 2 * local_width :].astype(jnp.bfloat16)
    query_normed = head_norm(queries, q_gain)
    key_normed = head_norm(key_rows, k_gain)
    images = token_count // IMG_TOKENS
    shaped = (images, IMG_TOKENS, local_width // HEAD_DIM, HEAD_DIM)
    context = attend(
        query_normed.reshape(shaped), key_normed.reshape(shaped), value_cast.reshape(shaped)
    )
    context = context.reshape(token_count, local_width)
    out_full = lax.all_gather(out_weight, "dp", axis=0, tiled=True)
    return lax.psum_scatter(
        lax.dot_general(
            context, out_full, (((1,), (1,)), ((), ())), preferred_element_type=jnp.float32
        ).astype(jnp.bfloat16),
        "mp",
        scatter_dimension=0,
        tiled=True,
    )


MESH = pl.DeviceIdType.MESH


def exchange_kernel(
    pairs, groups, tokens, ln_gain, q_w, k_w, v_w, q_gain, k_gain, out_w, result,
    raw, normed, weights, out_rows, context, partial, arrived, summed, final,
    local_sem, up_send, down_send, token_recv, peer_send, peer_recv,
    w_send, w_recv, own_send, own_recv, pass_send, pass_recv, out_send, out_recv,
    c_up, c_down, c_recv, p_send, p_recv, f_send, f_recv,
):
    dp = lax.axis_index("dp")
    group = lax.axis_index("mp")
    pair = dp // 2
    core = dp % 2
    rows = tokens.shape[0]
    part = rows // groups
    shard = q_w.shape[0]
    width = q_w.shape[1] // pairs
    span = 2 * shard
    heads = width // HEAD_DIM

    def at_pair(other):
        return (other * 2 + core, group)

    partner = (pair * 2 + (1 - core), group)

    def at_group(other):
        return (dp, other)

    def remote(source, target, send, recv, device):
        return pltpu.make_async_remote_copy(
            src_ref=source, dst_ref=target, send_sem=send, recv_sem=recv,
            device_id=device, device_id_type=MESH,
        )

    greeted = pltpu.get_barrier_semaphore()
    for step in range(1, pairs):
        pl.semaphore_signal(
            greeted, inc=1, device_id=at_pair((pair + step) % pairs), device_id_type=MESH
        )
    for step in range(1, groups):
        pl.semaphore_signal(
            greeted, inc=1, device_id=at_group((group + step) % groups), device_id_type=MESH
        )
    pl.semaphore_signal(greeted, inc=1, device_id=partner, device_id_type=MESH)

    projections = (q_w, k_w, v_w)

    def columns(other, h, t):
        start = pl.multiple_of(other * width + h * HEAD_DIM, HEAD_DIM)
        return projections[t].at[:, pl.ds(start, HEAD_DIM)]

    def slot(h, block, side, t):
        return weights.at[h, block, side, :, pl.ds(t * HEAD_DIM, HEAD_DIM)]

    quarter = pl.ds(pl.multiple_of(group * part, part), part)
    locals_ = [pltpu.make_async_copy(tokens, raw.at[pair], local_sem.at[0])]
    locals_.append(pltpu.make_async_copy(out_w, out_rows.at[core], local_sem.at[1]))
    for h in range(heads):
        for t in range(3):
            locals_.append(
                pltpu.make_async_copy(
                    columns(pair, h, t), slot(h, pair, core, t), local_sem.at[2 + 3 * h + t]
                )
            )
    for copy in locals_:
        copy.start()
    pl.semaphore_wait(greeted, pairs + groups - 1)

    def first_hop(up):
        return remote(
            tokens.at[quarter, :], raw.at[pair, quarter, :],
            (up_send if up else down_send).at[pair], token_recv.at[pair],
            at_pair(pair + 1 if up else pair - 1),
        )

    def next_hop(block, up):
        return remote(
            raw.at[block, quarter, :], raw.at[block, quarter, :],
            (up_send if up else down_send).at[block], token_recv.at[block],
            at_pair(pair + 1 if up else pair - 1),
        )

    beside = group + 1 - 2 * (group % 2)
    across = (group + 2) % 4
    first = jnp.where(core == 0, beside, across)
    second = jnp.where(core == 0, across, beside)
    opposite = 3 - group

    def part_of(block, other):
        return raw.at[block, pl.ds(pl.multiple_of(other * part, part), part), :]

    def peer_copy(block, owner, place, other):
        there = part_of(block, owner)
        return remote(
            there, there, peer_send.at[block, place], peer_recv.at[block, owner], at_group(other)
        )

    def to_first(block):
        return peer_copy(block, group, 0, first)

    def to_second(block):
        return peer_copy(block, group, 1, second)

    def cross(block):
        return peer_copy(block, first, 2, second)

    def from_peer(block, owner):
        return peer_copy(block, owner, 0, first)

    def weight_to(other, h, t):
        return remote(
            columns(other, h, t), slot(h, pair, core, t),
            w_send.at[other, h, t], w_recv.at[pair, h, t], at_pair(other),
        )

    def weight_from(other, h, t):
        there = slot(h, other, core, t)
        return remote(there, there, w_send.at[other, h, t], w_recv.at[other, h, t], at_pair(other))

    def own_weight(h, t):
        return remote(
            columns(pair, h, t), slot(h, pair, core, t), own_send.at[h, t], own_recv.at[h, t], partner
        )

    def partner_weight(h, t):
        there = slot(h, pair, 1 - core, t)
        return remote(there, there, own_send.at[h, t], own_recv.at[h, t], partner)

    def pass_on(other, h):
        there = weights.at[h, other, core]
        return remote(there, there, pass_send.at[other, h], pass_recv.at[other, h], partner)

    def passed(other, h):
        there = weights.at[h, other, 1 - core]
        return remote(there, there, pass_send.at[other, h], pass_recv.at[other, h], partner)

    def out_over():
        return remote(out_w, out_rows.at[core], out_send, out_recv, partner)

    def out_back():
        there = out_rows.at[1 - core]
        return remote(there, there, out_send, out_recv, partner)

    has_up = pair + 1 < pairs
    has_down = pair > 0

    @pl.when(has_up)
    def _():
        first_hop(True).start()

    @pl.when(has_down)
    def _():
        first_hop(False).start()

    def send_weights(up, some):
        for h in some:
            for distance in range(pairs - 1, 0, -1) if h == 0 else range(1, pairs):
                other = pair + distance if up else pair - distance

                @pl.when(other < pairs if up else other >= 0)
                def _():
                    for t in range(3):
                        weight_to(other, h, t).start()

    @pl.when(pair == 0)
    def _():
        send_weights(True, range(1))

    @pl.when(pair == pairs - 1)
    def _():
        send_weights(False, range(1))

    for h in range(heads):
        for t in range(3):
            own_weight(h, t).start()

    def normalise(block):
        @pl.loop(0, rows // 16)
        def _(chunk):
            place = pl.ds(pl.multiple_of(chunk * 16, 16), 16)
            values = raw[block, place, :].astype(jnp.float32)
            average = jnp.mean(values, axis=-1, keepdims=True)
            centred = values - average
            variance = jnp.mean(centred * centred, axis=-1, keepdims=True)
            scaled = centred * lax.rsqrt(variance + epsilon) * ln_gain[...]
            scaled = scaled.astype(jnp.bfloat16)
            for p in range(pairs):
                normed[p, block, place, :] = scaled[:, p * span : (p + 1) * span]

    for copy in locals_:
        copy.wait()
    normalise(pair)

    def relay(block, up):
        next_hop(block, up).wait_recv()

        @pl.when(has_up if up else has_down)
        def _():
            next_hop(block, up).start()

        to_first(block).start()
        to_second(block).start()

    for distance in range(1, pairs):
        @pl.when(pair - distance >= 0)
        def _():
            relay(pair - distance, True)

        @pl.when(pair + distance < pairs)
        def _():
            relay(pair + distance, False)

        @pl.when(has_up & (pair == distance))
        def _():
            send_weights(True, range(1))

        @pl.when(has_down & (pair == pairs - 1 - distance))
        def _():
            send_weights(False, range(1))

    def cross_tokens(block):
        from_peer(block, first).wait_recv()
        cross(block).start()

    for distance in range(1, pairs):
        @pl.when(pair - distance >= 0)
        def _():
            cross_tokens(pair - distance)

        @pl.when(pair + distance < pairs)
        def _():
            cross_tokens(pair + distance)

        if distance == min(2, pairs - 1):
            send_weights(True, range(1, heads))
            send_weights(False, range(1, heads))


    out_over().start()

    def take_tokens(block):
        from_peer(block, second).wait_recv()
        from_peer(block, opposite).wait_recv()
        normalise(block)

    def pass_weights(h):
        @pl.loop(1, pairs)
        def _(k):
            block = (pair + k) % pairs
            for t in range(3):
                weight_from(block, h, t).wait_recv()
            pass_on(block, h).start()

    for distance in range(1, pairs):
        if distance == pairs - 1:
            pass_weights(0)

        @pl.when(pair - distance >= 0)
        def _():
            take_tokens(pair - distance)

        @pl.when(pair + distance < pairs)
        def _():
            take_tokens(pair + distance)

    def head_layer_norm(values, scale_gain):
        average = jnp.mean(values, axis=-1, keepdims=True)
        centred = values - average
        variance = jnp.mean(centred * centred, axis=-1, keepdims=True)
        return (centred * lax.rsqrt(variance + epsilon) * scale_gain).astype(jnp.bfloat16)

    def context_hop(block, image, h, up):
        there = context.at[block, image, :, pl.ds(h * HEAD_DIM, HEAD_DIM)]
        return remote(
            there, there,
            (c_up if up else c_down).at[block, image, h], c_recv.at[block, image, h],
            at_pair(pair + 1 if up else pair - 1),
        )

    def pass_context(image, h, distance):
        for up in (True, False):
            block = pair - distance if up else pair + distance

            @pl.when(block >= 0 if up else block < pairs)
            def _():
                context_hop(block, image, h, up).wait_recv()

                @pl.when(has_up if up else has_down)
                def _():
                    context_hop(block, image, h, up).start()

    for h in range(heads):
        if h > 0:
            pass_weights(h)
        for t in range(3):
            partner_weight(h, t).wait_recv()

        @pl.loop(1, pairs)
        def _(k):
            passed((pair + k) % pairs, h).wait_recv()

        lanes = slice(h * HEAD_DIM, (h + 1) * HEAD_DIM)

        @pl.loop(0, pairs)
        def _(image):
            total = None
            for p in range(pairs):
                product = jnp.dot(
                    normed[p, image], weights[h, p].reshape(span, 3 * HEAD_DIM),
                    preferred_element_type=jnp.float32,
                )
                total = product if total is None else total + product
            queries = head_layer_norm(total[:, :HEAD_DIM], q_gain[pair, :, lanes])
            key_rows = head_layer_norm(total[:, HEAD_DIM : 2 * HEAD_DIM], k_gain[pair, :, lanes])
            value_rows = total[:, 2 * HEAD_DIM :].astype(jnp.bfloat16)
            scores = lax.dot_general(
                queries, key_rows, (((1,), (1,)), ((), ())), preferred_element_type=jnp.float32
            ) * (1.0 / math.sqrt(HEAD_DIM))
            highest = jnp.max(scores, axis=-1, keepdims=True)
            spread = jnp.exp(scores - highest)
            probs = (spread / jnp.sum(spread, axis=-1, keepdims=True)).astype(jnp.bfloat16)
            mixed = jnp.dot(probs, value_rows, preferred_element_type=jnp.float32)
            context[pair, image, :, lanes] = mixed.astype(jnp.bfloat16)

            @pl.when(has_up)
            def _():
                context_hop(pair, image, h, True).start()

            @pl.when(has_down)
            def _():
                context_hop(pair, image, h, False).start()

            if h > 0:
                pass_context(image, h - 1, 1)

    for distance in range(1, pairs):
        @pl.loop(0, pairs)
        def _(image):
            for h in range(heads):
                hop = distance + (1 if h < heads - 1 else 0)
                if hop < pairs and not (distance == pairs - 1 and h == heads - 1):
                    pass_context(image, h, hop)

    def partial_to(image, step):
        other = (group + step) % groups
        return remote(
            partial.at[image, pl.ds(pl.multiple_of(other * part, part), part), :],
            arrived.at[image, group],
            p_send.at[image, step - 1], p_recv.at[image, group], at_group(other),
        )

    def partial_from(image, step):
        other = (group + step) % groups
        there = arrived.at[image, other]
        return remote(there, there, p_send.at[image, step - 1], p_recv.at[image, other], at_group(other))

    out_back().wait_recv()

    @pl.loop(0, pairs)
    def _(image):
        pass_context(image, heads - 1, pairs - 1)

        for c in range(2):
            total = None
            for p in range(pairs):
                product = lax.dot_general(
                    context[p, image], out_rows[c, :, p * width : (p + 1) * width],
                    (((1,), (1,)), ((), ())), preferred_element_type=jnp.float32,
                )
                total = product if total is None else total + product
            partial[image, :, c * shard : (c + 1) * shard] = total.astype(jnp.bfloat16)
        for step in range(1, groups):
            partial_to(image, step).start()

    def final_to(image):
        return remote(
            summed.at[image], final.at[pair], f_send.at[image], f_recv.at[pair], at_pair(image)
        )

    def final_from(other):
        return remote(
            final.at[other], final.at[other], f_send.at[other], f_recv.at[other], at_pair(other)
        )

    @pl.loop(0, pairs)
    def _(image):
        total = partial[image, quarter, :].astype(jnp.float32)
        for step in range(1, groups):
            partial_from(image, step).wait_recv()
            total = total + arrived[image, (group + step) % groups].astype(jnp.float32)
        summed[image] = total.astype(jnp.bfloat16)

        @pl.when(image != pair)
        def _():
            final_to(image).start()

        @pl.when(image == pair)
        def _():
            final[pair] = summed[image]

    @pl.loop(1, pairs)
    def _(k):
        final_from((pair + k) % pairs).wait_recv()

    for p in range(pairs):
        result[:, p * span : (p + 1) * span] = final[p]

    @pl.when(has_up)
    def _():
        first_hop(True).wait_send()

    @pl.when(has_down)
    def _():
        first_hop(False).wait_send()

    for h in range(heads):
        for t in range(3):
            own_weight(h, t).wait_send()
    out_over().wait_send()
    for distance in range(1, pairs):
        for up in (True, False):
            inside = pair - distance >= 0 if up else pair + distance < pairs
            block = pair - distance if up else pair + distance

            @pl.when(inside & (has_up if up else has_down))
            def _():
                next_hop(block, up).wait_send()

                @pl.loop(0, pairs)
                def _(image):
                    for h in range(heads):
                        context_hop(block, image, h, up).wait_send()

    @pl.loop(0, pairs)
    def _(image):
        @pl.when(has_up)
        def _():
            for h in range(heads):
                context_hop(pair, image, h, True).wait_send()

        @pl.when(has_down)
        def _():
            for h in range(heads):
                context_hop(pair, image, h, False).wait_send()

        for step in range(1, groups):
            partial_to(image, step).wait_send()

    @pl.loop(1, pairs)
    def _(k):
        block = (pair + k) % pairs
        for h in range(heads):
            for t in range(3):
                weight_to(block, h, t).wait_send()
            pass_on(block, h).wait_send()
        to_first(block).wait_send()
        to_second(block).wait_send()
        cross(block).wait_send()
        final_to(block).wait_send()


def exchanged_heads(pairs, groups, tokens, ln_gain, q_w, k_w, v_w, q_gain, k_gain, out_w):
    rows, features = tokens.shape
    shard, local_width = q_w.shape
    width = local_width // pairs
    heads = width // HEAD_DIM
    part = rows // groups
    dma = pltpu.SemaphoreType.DMA
    in_hbm = pl.BlockSpec(memory_space=pl.ANY)
    in_vmem = pl.BlockSpec(memory_space=pltpu.VMEM)
    bf16 = jnp.bfloat16
    return pl.pallas_call(
        functools.partial(exchange_kernel, pairs, groups),
        out_shape=jax.ShapeDtypeStruct((part, features), bf16),
        in_specs=[in_hbm, in_vmem, in_hbm, in_hbm, in_hbm, in_vmem, in_vmem, in_hbm],
        out_specs=in_vmem,
        scratch_shapes=[
            pltpu.VMEM((pairs, rows, features), bf16),
            pltpu.VMEM((pairs, pairs, rows, 2 * shard), bf16),
            pltpu.VMEM((heads, pairs, 2, shard, 3 * HEAD_DIM), bf16),
            pltpu.VMEM((2, shard, local_width), bf16),
            pltpu.VMEM((pairs, pairs, rows, width), bf16),
            pltpu.VMEM((pairs, rows, 2 * shard), bf16),
            pltpu.VMEM((pairs, groups, part, 2 * shard), bf16),
            pltpu.VMEM((pairs, part, 2 * shard), bf16),
            pltpu.VMEM((pairs, part, 2 * shard), bf16),
            dma((2 + 3 * heads,)), dma((pairs,)), dma((pairs,)), dma((pairs,)),
            dma((pairs, groups)), dma((pairs, groups)),
            dma((pairs, heads, 3)), dma((pairs, heads, 3)), dma((heads, 3)), dma((heads, 3)),
            dma((pairs, heads)), dma((pairs, heads)), dma, dma,
            dma((pairs, pairs, heads)), dma((pairs, pairs, heads)), dma((pairs, pairs, heads)),
            dma((pairs, groups)), dma((pairs, groups)), dma((pairs,)), dma((pairs,)),
        ],
        compiler_params=pltpu.CompilerParams(
            collective_id=0, has_side_effects=True, vmem_limit_bytes=60 * 1024 * 1024
        ),
    )(
        tokens, ln_gain.reshape(1, features), q_w, k_w, v_w,
        q_gain.reshape(pairs, 1, width), k_gain.reshape(pairs, 1, width), out_w,
    )


def on_device(tokens, ln_gain, q_w, k_w, v_w, q_gain, k_gain, out_w):
    devices = lax.axis_size("dp")
    groups = lax.axis_size("mp")
    pairs = devices // 2
    fits = (
        devices % 2 == 0
        and pairs > 1
        and groups == 4
        and q_w.shape[1] % (pairs * HEAD_DIM) == 0
        and q_w.shape[0] % 128 == 0
        and tokens.shape[0] == IMG_TOKENS
        and tokens.shape[0] % (16 * groups) == 0
        and pairs <= 4
        and q_w.shape[1] <= 2 * pairs * HEAD_DIM
    )
    if fits:
        return exchanged_heads(pairs, groups, tokens, ln_gain, q_w, k_w, v_w, q_gain, k_gain, out_w)
    return gathered_weights(tokens, ln_gain, q_w, k_w, v_w, q_gain, k_gain, out_w)


def solution(mesh):
    in_specs = (
        P("dp", None),
        P(),
        P("dp", "mp"),
        P("dp", "mp"),
        P("dp", "mp"),
        P("mp"),
        P("mp"),
        P("dp", "mp"),
    )
    out_specs = P(("dp", "mp"), None)
    return jax.shard_map(
        on_device, mesh=mesh, in_specs=in_specs, out_specs=out_specs, check_vma=False
    )
```
